32 devices in a mesh: groups: 2 (over y), space: 4 (over z), tm: 2 (over x), chan: 2 (over core).
Axes of the slice: x: 2, y: 2, z: 4, core: 2. Of those that a mesh axis runs over, the one named last changes fastest.
Arguments:
- hidden_states: bfloat16 [8, 4, 64, 512], P(('groups', 'tm'), 'space', None, 'chan'), parts along dimension 0, may hold values from -25 to 25
- first_gain: float32 [512], P('chan'), may hold values from 0.1 to 1.9
- second_gain: float32 [512], P('chan'), may hold values from 0.1 to 1.9
- query_weight: bfloat16 [512, 512], replicated, may hold values from -0.4861359 to 0.4861359
- key_weight: bfloat16 [512, 512], replicated, may hold values from -0.4861359 to 0.4861359
- value_weight: bfloat16 [512, 512], replicated, may hold values from -0.25 to 0.25
- out_weight: bfloat16 [512, 512], replicated, may hold values from -0.25 to 0.25
- conv_kernel: bfloat16 [3, 3, 3, 512, 512], P(None, None, None, 'tm', 'chan'), may hold values from -0.0546875 to 0.0546875
Outputs:
- attended: bfloat16 [8, 4, 64, 512], P(('groups', 'tm'), 'space', None, 'chan'), parts along dimension 0
- convolved: bfloat16 [8, 4, 64, 512], P(('groups', 'tm'), 'space', None, 'chan'), parts along dimension 0
The draws below stay inside these ranges and needn't reach their ends.
There are 2 independent parts, one for each index of `groups`. The reference program is written for one: setup_inputs(seed, part) draws one part's arguments, and reference() takes and returns one part's arrays. A program takes and returns all parts, laid end to end along the dimension named above; an argument that names none is the same for every part. Nothing has to cross between parts.
All inputs are finite; a program needn't handle non-finite values.
Results may differ from the reference program's by a relative error of at most 0.012.
The reference program's roundings to bfloat16 on the way count: a program that leaves them out, or rounds other values in their place, can miss the bound.
Values may be sent and summed in bfloat16 or wider, within the bound.
A program may use at most 64 MiB of HBM per device.

```python
import jax
import jax.numpy as jnp
from jax import lax

D = 512
NGROUP = 32
W = 64
NF = 4
NH = 4


def draw_hidden_states(key, part):
    normal_key = jax.random.fold_in(key, 1)
    channel_key = jax.random.fold_in(key, 2)
    jitter_key = jax.random.fold_in(key, 3)
    frame_pos = jnp.arange(NF, dtype=jnp.float32) / (NF - 1)
    row_pos = jnp.arange(NH, dtype=jnp.float32) / (NH - 1)
    exponent = 0.5 * frame_pos[:, None] + 0.5 * row_pos[None, :] - 1.0
    jitter = jax.random.uniform(jitter_key, (NF, NH, W), minval=-0.1, maxval=0.1)
    token_scale = 10.0 ** (exponent[:, :, None] + jitter)
    channel_scale = jnp.exp(jax.random.uniform(channel_key, (D,), minval=jnp.log(0.5), maxval=jnp.log(5.0)))
    base = jnp.clip(jax.random.normal(normal_key, (NF, NH, W, D)), -3.5, 3.5)
    return (base * token_scale[:, :, :, None] * channel_scale).astype(jnp.bfloat16)


def drawn_pair(key):
    first = jnp.clip(jax.random.normal(jax.random.fold_in(key, 12), (D, D)), -4.5, 4.5)
    second = jnp.clip(jax.random.normal(jax.random.fold_in(key, 13), (D, D)), -4.5, 4.5)
    return (first, second)


def draw_query_weight(key, part):
    first, second = drawn_pair(key)
    result = first
    return (result * D ** (-0.5)).astype(jnp.bfloat16)


def draw_key_weight(key, part):
    first, second = drawn_pair(key)
    result = second
    return (result * D ** (-0.5)).astype(jnp.bfloat16)


def block_scale(own_key, extent, split, smallest, largest):
    def one(dim, parts):
        draws = jax.random.uniform(jax.random.fold_in(jax.random.fold_in(own_key, 6), dim), (parts,), jnp.float32, smallest / len(split), largest / len(split))
        return jnp.repeat(jnp.exp(draws), extent[dim] // parts).reshape((-1,) + (1,) * (len(extent) - dim - 1))

    loudness = one(*split[0])
    for cut in split[1:]:
        loudness = loudness * one(*cut)
    return loudness


def gaussian(rng, extent, scale, limit, split=(), held_as=jnp.bfloat16):
    gain = block_scale(rng, extent, split, -0.22, 0.18) if split else 1.0
    drawn = jax.random.normal(rng, extent, jnp.float32) * scale * gain
    return jnp.minimum(jnp.maximum(drawn, -limit), limit).astype(held_as)


def setup_inputs(seed: int = 0, part: int = 0) -> dict:
    arg_keys = jax.random.split(jax.random.key(seed), 9)
    own_keys = jax.random.split(jax.random.fold_in(arg_keys[8], part), 9)
    return {
        "hidden_states": draw_hidden_states(jax.random.fold_in(jax.random.fold_in(arg_keys[8], part), 71), part),
        "first_gain": jnp.clip(1.0 + 0.18 * jax.random.normal(arg_keys[1], (D,), jnp.float32), 0.1, 1.9),
        "second_gain": jnp.clip(1.0 + 0.18 * jax.random.normal(arg_keys[2], (D,), jnp.float32), 0.1, 1.9),
        "query_weight": draw_query_weight(jax.random.fold_in(arg_keys[8], 71), part),
        "key_weight": draw_key_weight(jax.random.fold_in(arg_keys[8], 71), part),
        "value_weight": gaussian(arg_keys[5], (D, D), D ** -0.5, 0.25),
        "out_weight": gaussian(arg_keys[6], (D, D), D ** -0.5, 0.25),
        "conv_kernel": gaussian(arg_keys[7], (3, 3, 3, D, D), (27 * D) ** -0.5, 0.0546875, ((3, 2), (4, 2))),
    }


EPSILON = 1e-06

def group_norm(source, gain_vector):
    grouped = source.reshape(-1, NGROUP, D // NGROUP)
    centre = lax.optimization_barrier(jnp.mean(grouped, axis=(0, 2)))
    shifted = grouped - centre[None, :, None]
    spread = lax.optimization_barrier(jnp.mean(shifted * shifted, axis=(0, 2)))
    scaled = shifted * lax.rsqrt(spread + EPSILON)[None, :, None]
    return scaled.reshape(source.shape) * gain_vector

def reference(hidden_states, first_gain, second_gain, query_weight, key_weight, value_weight, out_weight, conv_kernel):
    source = hidden_states.astype(jnp.float32)
    normed = group_norm(source, first_gain).astype(jnp.bfloat16)
    frame_tokens = normed.reshape(NF, NH * W, D)

    def frame_attention(tokens):
        queries = jnp.dot(tokens, query_weight, preferred_element_type=jnp.float32).astype(jnp.bfloat16)
        keyed = jnp.dot(tokens, key_weight, preferred_element_type=jnp.float32).astype(jnp.bfloat16)
        valued = jnp.dot(tokens, value_weight, preferred_element_type=jnp.float32).astype(jnp.bfloat16)
        scores = jnp.dot(queries, keyed.T, preferred_element_type=jnp.float32) * D ** (-0.5)
        peaked = lax.optimization_barrier(jnp.max(scores, axis=1))
        weights = jnp.exp(scores - peaked[:, None])
        mass = lax.optimization_barrier(jnp.sum(weights, axis=1))
        mixed = jnp.dot(weights.astype(jnp.bfloat16), valued, preferred_element_type=jnp.float32)
        mixed = (mixed / mass[:, None]).astype(jnp.bfloat16)
        return jnp.dot(mixed, out_weight, preferred_element_type=jnp.float32).astype(jnp.bfloat16)
    attended = lax.map(frame_attention, frame_tokens).reshape(source.shape)
    resid = source + attended.astype(jnp.float32)
    activated = jax.nn.silu(group_norm(resid, second_gain)).astype(jnp.bfloat16)
    convolved = lax.conv_general_dilated(activated.astype(jnp.float32)[None], conv_kernel.astype(jnp.float32), (1, 1, 1), [(2, 0), (1, 1), (1, 1)], dimension_numbers=('NDHWC', 'DHWIO', 'NDHWC'), precision=lax.Precision.HIGHEST)[0]
    return (attended, convolved.astype(jnp.bfloat16))
```

```python
import functools

import jax
import jax.numpy as jnp
from jax import lax
from jax.experimental import pallas as pl
from jax.experimental.pallas import tpu as pltpu
from jax.sharding import PartitionSpec as P

D = 512
NGROUP = 32
EPSILON = 1e-06
LANES = 128
BLOCKS = D // LANES
GROUP = D // NGROUP
MESH = pl.DeviceIdType.MESH
F32 = jnp.float32
BF16 = jnp.bfloat16


def group_total(v):
    lane = lax.broadcasted_iota(jnp.int32, v.shape, 1)
    width = v.shape[1]
    step = 1
    while step < GROUP:
        above = pltpu.roll(v, width - step, 1)
        below = pltpu.roll(v, step, 1)
        v = v + jnp.where((lane // step) % 2 == 0, above, below)
        step *= 2
    return v


def packed_moments(values, first_block):
    sums = jnp.sum(values, axis=0, keepdims=True)
    squares = jnp.sum(values * values, axis=0, keepdims=True)
    rows = jnp.concatenate([sums, squares] * 4, axis=0)
    totals = group_total(rows)
    place = lax.broadcasted_iota(jnp.int32, (1, LANES), 1) % GROUP
    packed = jnp.zeros((1, LANES), F32)
    for block in range(values.shape[1] // LANES):
        piece = totals[:, block * LANES : (block + 1) * LANES]
        packed = jnp.where(place == first_block + block, piece[0:1], packed)
        packed = jnp.where(place == BLOCKS + first_block + block, piece[1:2], packed)
    return packed


def moments(packed, population):
    place = lax.broadcasted_iota(jnp.int32, (2 * BLOCKS, LANES), 1) % GROUP
    row = lax.broadcasted_iota(jnp.int32, (2 * BLOCKS, LANES), 0)
    wide = jnp.broadcast_to(packed, (2 * BLOCKS, LANES))
    spread_out = group_total(jnp.where(place == row, wide, 0.0)) / population
    mean = jnp.concatenate([spread_out[k : k + 1] for k in range(BLOCKS)], axis=1)
    square = jnp.concatenate([spread_out[BLOCKS + k : BLOCKS + k + 1] for k in range(BLOCKS)], axis=1)
    variance = jnp.maximum(square - mean * mean, 0.0)
    return mean, lax.rsqrt(variance + EPSILON)


def kernel(
    S, T, C, W,
    x, g1, g2, wq_hbm, wk_hbm, wv_hbm, wo_hbm, wc_hbm,
    att_out, conv_out,
    wq, wk, wv, wo, wc,
    stat1_src, stat1, stat2_src, stat2, gall1, gall2,
    xall, tokens, att_src, att_in, dsrc, dall, act, part_src, part,
    wsem, send_sem, gsem, s1sem, xsem, s2sem, asem, dsem, psend, psem,
):
    g = lax.axis_index("groups")
    h = lax.axis_index("space")
    t = lax.axis_index("tm")
    c = lax.axis_index("chan")
    n = S * T * C
    me = (h * T + t) * C + c
    half = D // C
    Kc = D // T
    NF = T * C
    other = lax.rem(c + 1, C)

    def place(i):
        return (g, i // (T * C), lax.rem(i // C, T), lax.rem(i, C))

    loads = [
        pltpu.make_async_copy(src, dst, wsem.at[i])
        for i, (src, dst) in enumerate(
            [(wk_hbm, wk), (wq_hbm, wq), (wv_hbm, wv), (wo_hbm, wo), (wc_hbm, wc)]
        )
    ]
    for load in loads:
        load.start()

    barrier = pltpu.get_barrier_semaphore()

    @pl.loop(1, n)
    def _(i):
        pl.semaphore_signal(barrier, inc=1, device_id=place(lax.rem(me + i, n)), device_id_type=MESH)

    own = x[...].reshape(C * W, half).astype(F32)
    stat1_src[...] = packed_moments(own, c * (half // LANES))
    gall1[c] = g1[...]
    gall2[c] = g2[...]
    stat1[me] = stat1_src[...]
    xall[h * C + c] = x[c, 0]
    pl.semaphore_wait(barrier, n - 1)

    def send_stat(src, dst, sends, recvs):
        @pl.loop(1, n)
        def _(i):
            pltpu.make_async_remote_copy(
                src_ref=src, dst_ref=dst.at[me], send_sem=sends, recv_sem=recvs,
                device_id=place(lax.rem(me + i, n)), device_id_type=MESH,
            ).start()

    def drain(ref, sem):
        pltpu.make_async_copy(ref, ref, sem).wait()

    send_stat(stat1_src, stat1, send_sem.at[0], s1sem)
    gains = [
        pltpu.make_async_remote_copy(
            src_ref=src, dst_ref=dst.at[c], send_sem=send_sem.at[1 + k], recv_sem=gsem.at[k],
            device_id=(g, h, t, other), device_id_type=MESH,
        )
        for k, (src, dst) in enumerate([(g1, gall1), (g2, gall2)])
    ]
    for copy in gains:
        copy.start()
    for dh in list(range(1, S)) + [0]:
        for dc in range(C):
            if dh == 0 and dc == 0:
                continue
            frame = lax.rem(c + dc, C)
            pltpu.make_async_remote_copy(
                src_ref=x.at[frame, 0], dst_ref=xall.at[h * C + c],
                send_sem=send_sem.at[3], recv_sem=xsem,
                device_id=(g, lax.rem(h + dh, S), t, frame), device_id_type=MESH,
            ).start()

    drain(stat1.at[pl.ds(0, n - 1)], s1sem)
    for copy in gains:
        copy.wait()
    population = float(n * W * GROUP)
    mean1, scale1 = moments(jnp.sum(stat1[...], axis=0), population)
    gain1 = jnp.concatenate([gall1[k] for k in range(C)], axis=1)
    gain2 = jnp.concatenate([gall2[k] for k in range(C)], axis=1)

    drain(xall.at[pl.ds(0, S * C - 1)], xsem)

    @pl.loop(0, S, unroll=S <= 4)
    def _(r):
        for k in range(C):
            lanes = slice(k * half, (k + 1) * half)
            value = xall[r * C + k].astype(F32)
            value = (value - mean1[:, lanes]) * scale1[:, lanes] * gain1[:, lanes]
            tokens[r, :, lanes] = value.astype(BF16)

    mine = tokens[h]
    every = tokens[...].reshape(S * W, D)
    loads[0].wait()
    keyed = jnp.dot(every, wk[...], preferred_element_type=F32).astype(BF16)
    loads[1].wait()
    queries = jnp.dot(mine, wq[...], preferred_element_type=F32).astype(BF16)
    scores = lax.dot_general(
        queries, keyed, (((1,), (1,)), ((), ())), preferred_element_type=F32
    ) * (D ** (-0.5))
    loads[2].wait()
    valued = jnp.dot(every, wv[...], preferred_element_type=F32).astype(BF16)
    weights = jnp.exp(scores - jnp.max(scores, axis=1, keepdims=True))
    mass = jnp.sum(weights, axis=1, keepdims=True)
    mixed = jnp.dot(weights.astype(BF16), valued, preferred_element_type=F32)
    mixed = (mixed / mass).astype(BF16)
    loads[3].wait()
    attended = jnp.dot(mixed, wo[...], preferred_element_type=F32).astype(BF16)

    source = jnp.concatenate([xall[h * C + k] for k in range(C)], axis=1).astype(F32)
    resid = (source - mean1) + attended.astype(F32)
    for k in range(T):
        dsrc[k] = resid[:, k * Kc : (k + 1) * Kc].astype(BF16)
    for k in range(C):
        att_src[k] = attended[:, k * half : (k + 1) * half]
    stat2_src[...] = packed_moments(resid, 0)
    stat2[me] = stat2_src[...]
    send_stat(stat2_src, stat2, send_sem.at[4], s2sem)

    frame_at = t * C + c

    def send_rows(dh, skip_self):
        for dt in range(T):
            for dc in range(C):
                if skip_self and dt == 0 and dc == 0:
                    continue
                to = lax.rem(t + dt, T)
                pltpu.make_async_remote_copy(
                    src_ref=dsrc.at[to], dst_ref=dall.at[1 - dh, frame_at],
                    send_sem=send_sem.at[6 + dh], recv_sem=dsem.at[1 - dh],
                    device_id=(g, h + dh, to, lax.rem(c + dc, C)), device_id_type=MESH,
                ).start()

    @pl.when(h > 0)
    def _():
        send_rows(-1, False)

    @pl.when(h < S - 1)
    def _():
        send_rows(1, False)

    send_rows(0, True)
    back = pltpu.make_async_remote_copy(
        src_ref=att_src.at[other], dst_ref=att_in, send_sem=send_sem.at[8], recv_sem=asem,
        device_id=(g, h, t, other), device_id_type=MESH,
    )
    back.start()
    dall[1, frame_at] = dsrc[t]
    att_out[c, 0] = att_src[c]
    act[0:2] = jnp.zeros((2,) + act.shape[1:], BF16)

    drain(stat2.at[pl.ds(0, n - 1)], s2sem)
    mean2, scale2 = moments(jnp.sum(stat2[...], axis=0), population)
    factor = scale2 * gain2

    def sliced(v):
        out = v[:, 0:Kc]
        for k in range(1, T):
            out = jnp.where(t == k, v[:, k * Kc : (k + 1) * Kc], out)
        return out

    mean_t = sliced(mean2)
    factor_t = sliced(factor)
    column = lax.broadcasted_iota(jnp.int32, (W, Kc), 0)

    def activate(row):
        @pl.loop(0, NF, unroll=NF <= 4)
        def _(f):
            v = (dall[row, f].astype(F32) - mean_t) * factor_t
            a = v / (1.0 + jnp.exp(-v))
            left = jnp.where(column == 0, 0.0, pltpu.roll(a, 1, 0))
            right = jnp.where(column == W - 1, 0.0, pltpu.roll(a, W - 1, 0))
            for e, piece in enumerate((left, a, right)):
                k = row * 3 + e
                act[f + 2, :, k * Kc : (k + 1) * Kc] = piece.astype(BF16)

    def blank(row):
        act[2:, :, row * 3 * Kc : (row + 1) * 3 * Kc] = jnp.zeros((NF, W, 3 * Kc), BF16)

    drain(dall.at[1, pl.ds(0, NF - 1)], dsem.at[1])
    activate(1)

    @pl.when(h > 0)
    def _():
        drain(dall.at[0], dsem.at[0])
        activate(0)

    @pl.when(h == 0)
    def _():
        blank(0)

    @pl.when(h < S - 1)
    def _():
        drain(dall.at[2], dsem.at[2])
        activate(2)

    @pl.when(h == S - 1)
    def _():
        blank(2)

    loads[4].wait()

    def partial(to):
        total = None
        for a in range(3):
            window = act[pl.ds(to * C + a, C)].reshape(C * W, 9 * Kc)
            product = jnp.dot(window, wc[a], preferred_element_type=F32)
            total = product if total is None else total + product
        return total

    returns = []
    for dt in range(1, T):
        to = lax.rem(t + dt, T)
        part_src[dt - 1] = partial(to)
        copy = pltpu.make_async_remote_copy(
            src_ref=part_src.at[dt - 1], dst_ref=part.at[dt - 1],
            send_sem=psend.at[dt - 1], recv_sem=psem.at[dt - 1],
            device_id=(g, h, to, c), device_id_type=MESH,
        )
        copy.start()
        returns.append(copy)
    total = partial(t)
    back.wait()
    att_out[other, 0] = att_in[...]

    drain(stat1.at[pl.ds(0, n - 1)], send_sem.at[0])
    drain(xall.at[pl.ds(0, S * C - 1)], send_sem.at[3])
    drain(stat2.at[pl.ds(0, n - 1)], send_sem.at[4])
    drain(dall.at[1, pl.ds(0, NF - 1)], send_sem.at[6])

    @pl.when(h > 0)
    def _():
        drain(dall.at[0], send_sem.at[5])

    @pl.when(h < S - 1)
    def _():
        drain(dall.at[2], send_sem.at[7])

    for k, copy in enumerate(returns):
        copy.wait()
        total = total + part[k]
    conv_out[...] = total.reshape(conv_out.shape).astype(BF16)


def on_device(S, T, C, x, g1, g2, wq, wk, wv, wo, wc):
    frames, rows, W, half = x.shape
    assert frames == C and rows == 1 and half * C == D
    Kc = wc.shape[3]
    assert Kc * T == D
    n, NF = S * T * C, T * C
    wc = wc.reshape(3, 9 * Kc, half)
    vmem = pl.BlockSpec(memory_space=pltpu.VMEM)
    hbm = pl.BlockSpec(memory_space=pl.ANY)
    out = jax.ShapeDtypeStruct(x.shape, BF16)
    dma = pltpu.SemaphoreType.DMA
    return pl.pallas_call(
        functools.partial(kernel, S, T, C, W),
        out_shape=(out, out),
        in_specs=[vmem] * 3 + [hbm] * 5,
        out_specs=(vmem, vmem),
        scratch_shapes=[
            *[pltpu.VMEM((D, D), BF16)] * 4,
            pltpu.VMEM(wc.shape, BF16),
            pltpu.VMEM((1, LANES), F32),
            pltpu.VMEM((n, 1, LANES), F32),
            pltpu.VMEM((1, LANES), F32),
            pltpu.VMEM((n, 1, LANES), F32),
            pltpu.VMEM((C, 1, half), F32),
            pltpu.VMEM((C, 1, half), F32),
            pltpu.VMEM((S * C, W, half), BF16),
            pltpu.VMEM((S, W, D), BF16),
            pltpu.VMEM((C, W, half), BF16),
            pltpu.VMEM((W, half), BF16),
            pltpu.VMEM((T, W, Kc), BF16),
            pltpu.VMEM((3, NF, W, Kc), BF16),
            pltpu.VMEM((NF + 2, W, 9 * Kc), BF16),
            pltpu.VMEM((max(T - 1, 1), C * W, half), F32),
            pltpu.VMEM((max(T - 1, 1), C * W, half), F32),
            dma((5,)),
            dma((9,)),
            dma((2,)),
            dma(()),
            dma(()),
            dma(()),
            dma(()),
            dma((3,)),
            dma((max(T - 1, 1),)),
            dma((max(T - 1, 1),)),
        ],
        compiler_params=pltpu.CompilerParams(collective_id=0, has_side_effects=True),
    )(x, g1.reshape(1, half), g2.reshape(1, half), wq, wk, wv, wo, wc)


def solution(mesh):
    S, T, C = mesh.shape["space"], mesh.shape["tm"], mesh.shape["chan"]
    placed = (
        P(("groups", "tm"), "space", None, "chan"),
        P("chan"),
        P("chan"),
        P(),
        P(),
        P(),
        P(),
        P(None, None, None, "tm", "chan"),
    )
    return jax.shard_map(
        functools.partial(on_device, S, T, C),
        mesh=mesh,
        in_specs=placed,
        out_specs=(
            P(("groups", "tm"), "space", None, "chan"),
            P(("groups", "tm"), "space", None, "chan"),
        ),
        check_vma=False,
    )
```

```python
import functools

import jax
import jax.numpy as jnp
from jax import lax
from jax.experimental import pallas as pl
from jax.experimental.pallas import tpu as pltpu
from jax.sharding import PartitionSpec as P

D = 512
NGROUP = 32
EPSILON = 1e-06
LANES = 128
BLOCKS = D // LANES
GROUP = D // NGROUP
MESH = pl.DeviceIdType.MESH
F32 = jnp.float32
BF16 = jnp.bfloat16


def group_total(v):
    lane = lax.broadcasted_iota(jnp.int32, v.shape, 1)
    width = v.shape[1]
    step = 1
    while step < GROUP:
        above = pltpu.roll(v, width - step, 1)
        below = pltpu.roll(v, step, 1)
        v = v + jnp.where((lane // step) % 2 == 0, above, below)
        step *= 2
    return v


def packed_moments(values, first_block):
    sums = jnp.sum(values, axis=0, keepdims=True)
    squares = jnp.sum(values * values, axis=0, keepdims=True)
    rows = jnp.concatenate([sums, squares] * 4, axis=0)
    totals = group_total(rows)
    place = lax.broadcasted_iota(jnp.int32, (1, LANES), 1) % GROUP
    packed = jnp.zeros((1, LANES), F32)
    for block in range(values.shape[1] // LANES):
        piece = totals[:, block * LANES : (block + 1) * LANES]
        packed = jnp.where(place == first_block + block, piece[0:1], packed)
        packed = jnp.where(place == BLOCKS + first_block + block, piece[1:2], packed)
    return packed


def moments(packed, population):
    place = lax.broadcasted_iota(jnp.int32, (2 * BLOCKS, LANES), 1) % GROUP
    row = lax.broadcasted_iota(jnp.int32, (2 * BLOCKS, LANES), 0)
    wide = jnp.broadcast_to(packed, (2 * BLOCKS, LANES))
    spread_out = group_total(jnp.where(place == row, wide, 0.0)) / population
    mean = jnp.concatenate([spread_out[k : k + 1] for k in range(BLOCKS)], axis=1)
    square = jnp.concatenate([spread_out[BLOCKS + k : BLOCKS + k + 1] for k in range(BLOCKS)], axis=1)
    variance = jnp.maximum(square - mean * mean, 0.0)
    return mean, lax.rsqrt(variance + EPSILON)


def kernel(
    S, T, C, W,
    x_hbm, g1, g2, wq_hbm, wk_hbm, wv_hbm, wo_hbm, wc_hbm,
    att_out, conv_out,
    x, wq, wk, wv, wo, wc,
    stat1_src, stat1, stat2_src, stat2, gall1, gall2,
    xall, tokens, att_src, att_in, dsrc, dall, act, part_src, part,
    xload, wsem, send_sem, gsem, s1sem, xsem, s2sem, asem, dsem, psend, psem,
):
    g = lax.axis_index("groups")
    h = lax.axis_index("space")
    t = lax.axis_index("tm")
    c = lax.axis_index("chan")
    n = S * T * C
    me = (h * T + t) * C + c
    half = D // C
    Kc = D // T
    NF = T * C
    other = lax.rem(c + 1, C)

    def place(i):
        return (g, i // (T * C), lax.rem(i // C, T), lax.rem(i, C))

    first = [
        pltpu.make_async_copy(src, dst, xload.at[i])
        for i, (src, dst) in enumerate([(x_hbm, x), (g1, gall1.at[c]), (g2, gall2.at[c])])
    ]
    for load in first:
        load.start()
    barrier = pltpu.get_barrier_semaphore()

    @pl.loop(1, n)
    def _(i):
        pl.semaphore_signal(barrier, inc=1, device_id=place(lax.rem(me + i, n)), device_id_type=MESH)

    loads = [
        pltpu.make_async_copy(src, dst, wsem.at[i])
        for i, (src, dst) in enumerate(
            [(wk_hbm, wk), (wq_hbm, wq), (wv_hbm, wv), (wo_hbm, wo), (wc_hbm, wc)]
        )
    ]
    for load in loads:
        load.start()

    for load in first:
        load.wait()
    own = x[...].reshape(C * W, half).astype(F32)
    stat1_src[...] = packed_moments(own, c * (half // LANES))
    stat1[me] = stat1_src[...]
    xall[h * C + c] = x[c, 0]
    pl.semaphore_wait(barrier, n - 1)

    def send_stat(src, dst, sends, recvs):
        @pl.loop(1, n)
        def _(i):
            pltpu.make_async_remote_copy(
                src_ref=src, dst_ref=dst.at[me], send_sem=sends, recv_sem=recvs,
                device_id=place(lax.rem(me + i, n)), device_id_type=MESH,
            ).start()

    def drain(ref, sem):
        pltpu.make_async_copy(ref, ref, sem).wait()

    send_stat(stat1_src, stat1, send_sem.at[0], s1sem)
    gains = [
        pltpu.make_async_remote_copy(
            src_ref=src, dst_ref=dst.at[c], send_sem=send_sem.at[1 + k], recv_sem=gsem.at[k],
            device_id=(g, h, t, other), device_id_type=MESH,
        )
        for k, (src, dst) in enumerate([(g1, gall1), (g2, gall2)])
    ]
    for copy in gains:
        copy.start()
    for dh in list(range(1, S)) + [0]:
        for dc in range(C):
            if dh == 0 and dc == 0:
                continue
            frame = lax.rem(c + dc, C)
            pltpu.make_async_remote_copy(
                src_ref=x.at[frame, 0], dst_ref=xall.at[h * C + c],
                send_sem=send_sem.at[3], recv_sem=xsem,
                device_id=(g, lax.rem(h + dh, S), t, frame), device_id_type=MESH,
            ).start()

    drain(stat1.at[pl.ds(0, n - 1)], s1sem)
    for copy in gains:
        copy.wait()
    population = float(n * W * GROUP)
    mean1, scale1 = moments(jnp.sum(stat1[...], axis=0), population)
    gain1 = jnp.concatenate([gall1[k] for k in range(C)], axis=1)
    gain2 = jnp.concatenate([gall2[k] for k in range(C)], axis=1)

    drain(xall.at[pl.ds(0, S * C - 1)], xsem)

    @pl.loop(0, S, unroll=S <= 4)
    def _(r):
        for k in range(C):
            lanes = slice(k * half, (k + 1) * half)
            value = xall[r * C + k].astype(F32)
            value = (value - mean1[:, lanes]) * scale1[:, lanes] * gain1[:, lanes]
            tokens[r, :, lanes] = value.astype(BF16)

    mine = tokens[h]
    every = tokens[...].reshape(S * W, D)
    loads[0].wait()
    keyed = jnp.dot(every, wk[...], preferred_element_type=F32).astype(BF16)
    loads[1].wait()
    queries = jnp.dot(mine, wq[...], preferred_element_type=F32).astype(BF16)
    scores = lax.dot_general(
        queries, keyed, (((1,), (1,)), ((), ())), preferred_element_type=F32
    ) * (D ** (-0.5))
    loads[2].wait()
    valued = jnp.dot(every, wv[...], preferred_element_type=F32).astype(BF16)
    weights = jnp.exp(scores - jnp.max(scores, axis=1, keepdims=True))
    mass = jnp.sum(weights, axis=1, keepdims=True)
    mixed = jnp.dot(weights.astype(BF16), valued, preferred_element_type=F32)
    mixed = (mixed / mass).astype(BF16)
    loads[3].wait()
    attended = jnp.dot(mixed, wo[...], preferred_element_type=F32).astype(BF16)

    source = jnp.concatenate([xall[h * C + k] for k in range(C)], axis=1).astype(F32)
    resid = (source - mean1) + attended.astype(F32)
    for k in range(T):
        dsrc[k] = resid[:, k * Kc : (k + 1) * Kc].astype(BF16)
    for k in range(C):
        att_src[k] = attended[:, k * half : (k + 1) * half]
    stat2_src[...] = packed_moments(resid, 0)
    stat2[me] = stat2_src[...]
    send_stat(stat2_src, stat2, send_sem.at[4], s2sem)

    frame_at = t * C + c

    def send_rows(dh, skip_self):
        for dt in range(T):
            for dc in range(C):
                if skip_self and dt == 0 and dc == 0:
                    continue
                to = lax.rem(t + dt, T)
                pltpu.make_async_remote_copy(
                    src_ref=dsrc.at[to], dst_ref=dall.at[1 - dh, frame_at],
                    send_sem=send_sem.at[6 + dh], recv_sem=dsem.at[1 - dh],
                    device_id=(g, h + dh, to, lax.rem(c + dc, C)), device_id_type=MESH,
                ).start()

    @pl.when(h > 0)
    def _():
        send_rows(-1, False)

    @pl.when(h < S - 1)
    def _():
        send_rows(1, False)

    send_rows(0, True)
    back = pltpu.make_async_remote_copy(
        src_ref=att_src.at[other], dst_ref=att_in, send_sem=send_sem.at[8], recv_sem=asem,
        device_id=(g, h, t, other), device_id_type=MESH,
    )
    back.start()
    dall[1, frame_at] = dsrc[t]
    att_out[c, 0] = att_src[c]
    act[0:2] = jnp.zeros((2,) + act.shape[1:], BF16)

    drain(stat2.at[pl.ds(0, n - 1)], s2sem)
    mean2, scale2 = moments(jnp.sum(stat2[...], axis=0), population)
    factor = scale2 * gain2

    def sliced(v):
        out = v[:, 0:Kc]
        for k in range(1, T):
            out = jnp.where(t == k, v[:, k * Kc : (k + 1) * Kc], out)
        return out

    mean_t = sliced(mean2)
    factor_t = sliced(factor)
    column = lax.broadcasted_iota(jnp.int32, (W, Kc), 0)

    def activate(row):
        @pl.loop(0, NF, unroll=NF <= 4)
        def _(f):
            v = (dall[row, f].astype(F32) - mean_t) * factor_t
            a = v / (1.0 + jnp.exp(-v))
            left = jnp.where(column == 0, 0.0, pltpu.roll(a, 1, 0))
            right = jnp.where(column == W - 1, 0.0, pltpu.roll(a, W - 1, 0))
            for e, piece in enumerate((left, a, right)):
                k = row * 3 + e
                act[f + 2, :, k * Kc : (k + 1) * Kc] = piece.astype(BF16)

    def blank(row):
        act[2:, :, row * 3 * Kc : (row + 1) * 3 * Kc] = jnp.zeros((NF, W, 3 * Kc), BF16)

    drain(dall.at[1, pl.ds(0, NF - 1)], dsem.at[1])
    activate(1)

    @pl.when(h > 0)
    def _():
        drain(dall.at[0], dsem.at[0])
        activate(0)

    @pl.when(h == 0)
    def _():
        blank(0)

    @pl.when(h < S - 1)
    def _():
        drain(dall.at[2], dsem.at[2])
        activate(2)

    @pl.when(h == S - 1)
    def _():
        blank(2)

    loads[4].wait()

    def partial(to):
        total = None
        for a in range(3):
            window = act[pl.ds(to * C + a, C)].reshape(C * W, 9 * Kc)
            product = jnp.dot(window, wc[a], preferred_element_type=F32)
            total = product if total is None else total + product
        return total

    returns = []
    for dt in range(1, T):
        to = lax.rem(t + dt, T)
        part_src[dt - 1] = partial(to).astype(BF16)
        copy = pltpu.make_async_remote_copy(
            src_ref=part_src.at[dt - 1], dst_ref=part.at[dt - 1],
            send_sem=psend.at[dt - 1], recv_sem=psem.at[dt - 1],
            device_id=(g, h, to, c), device_id_type=MESH,
        )
        copy.start()
        returns.append(copy)
    total = partial(t)
    back.wait()
    att_out[other, 0] = att_in[...]

    drain(stat1.at[pl.ds(0, n - 1)], send_sem.at[0])
    drain(xall.at[pl.ds(0, S * C - 1)], send_sem.at[3])
    drain(stat2.at[pl.ds(0, n - 1)], send_sem.at[4])
    drain(dall.at[1, pl.ds(0, NF - 1)], send_sem.at[6])

    @pl.when(h > 0)
    def _():
        drain(dall.at[0], send_sem.at[5])

    @pl.when(h < S - 1)
    def _():
        drain(dall.at[2], send_sem.at[7])

    for k, copy in enumerate(returns):
        copy.wait()
        total = total + part[k].astype(F32)
    conv_out[...] = total.reshape(conv_out.shape).astype(BF16)


def hand_over(att_in, conv_in, att_out, conv_out):
    att_out[...] = att_in[...]
    conv_out[...] = conv_in[...]


def on_device(S, T, C, x, g1, g2, wq, wk, wv, wo, wc):
    frames, rows, W, half = x.shape
    assert frames == C and rows == 1 and half * C == D
    Kc = wc.shape[3]
    assert Kc * T == D
    n, NF = S * T * C, T * C
    wc = wc.reshape(3, 9 * Kc, half)
    vmem = pl.BlockSpec(memory_space=pltpu.VMEM)
    hbm = pl.BlockSpec(memory_space=pl.ANY)
    out = jax.ShapeDtypeStruct(x.shape, BF16)
    dma = pltpu.SemaphoreType.DMA
    kept = pltpu.VMEM(x.shape, BF16)
    results = pl.pallas_call(
        functools.partial(kernel, S, T, C, W),
        out_shape=(kept, kept),
        in_specs=[hbm] * 8,
        out_specs=(vmem, vmem),
        scratch_shapes=[
            pltpu.VMEM(x.shape, BF16),
            *[pltpu.VMEM((D, D), BF16)] * 4,
            pltpu.VMEM(wc.shape, BF16),
            pltpu.VMEM((1, LANES), F32),
            pltpu.VMEM((n, 1, LANES), F32),
            pltpu.VMEM((1, LANES), F32),
            pltpu.VMEM((n, 1, LANES), F32),
            pltpu.VMEM((C, 1, half), F32),
            pltpu.VMEM((C, 1, half), F32),
            pltpu.VMEM((S * C, W, half), BF16),
            pltpu.VMEM((S, W, D), BF16),
            pltpu.VMEM((C, W, half), BF16),
            pltpu.VMEM((W, half), BF16),
            pltpu.VMEM((T, W, Kc), BF16),
            pltpu.VMEM((3, NF, W, Kc), BF16),
            pltpu.VMEM((NF + 2, W, 9 * Kc), BF16),
            pltpu.VMEM((max(T - 1, 1), C * W, half), BF16),
            pltpu.VMEM((max(T - 1, 1), C * W, half), BF16),
            dma((3,)),
            dma((5,)),
            dma((9,)),
            dma((2,)),
            dma(()),
            dma(()),
            dma(()),
            dma(()),
            dma((3,)),
            dma((max(T - 1, 1),)),
            dma((max(T - 1, 1),)),
        ],
        compiler_params=pltpu.CompilerParams(collective_id=0, has_side_effects=True),
    )(x, g1.reshape(1, half), g2.reshape(1, half), wq, wk, wv, wo, wc)
    return pl.pallas_call(
        hand_over, out_shape=(out, out), in_specs=[vmem] * 2, out_specs=(vmem, vmem),
    )(*[pltpu.with_memory_space_constraint(r, pltpu.VMEM) for r in results])


def solution(mesh):
    S, T, C = mesh.shape["space"], mesh.shape["tm"], mesh.shape["chan"]
    placed = (
        P(("groups", "tm"), "space", None, "chan"),
        P("chan"),
        P("chan"),
        P(),
        P(),
        P(),
        P(),
        P(None, None, None, "tm", "chan"),
    )
    return jax.shard_map(
        functools.partial(on_device, S, T, C),
        mesh=mesh,
        in_specs=placed,
        out_specs=(
            P(("groups", "tm"), "space", None, "chan"),
            P(("groups", "tm"), "space", None, "chan"),
        ),
        check_vma=False,
    )
```

```python
import functools

import jax
import jax.numpy as jnp
from jax import lax
from jax.experimental import pallas as pl
from jax.experimental.pallas import tpu as pltpu
from jax.sharding import PartitionSpec as P

D = 512
NGROUP = 32
EPSILON = 1e-06
LANES = 128
BLOCKS = D // LANES
GROUP = D // NGROUP
MESH = pl.DeviceIdType.MESH
REACH = 2
F32 = jnp.float32
BF16 = jnp.bfloat16


def group_total(v):
    lane = lax.broadcasted_iota(jnp.int32, v.shape, 1)
    width = v.shape[1]
    step = 1
    while step < GROUP:
        above = pltpu.roll(v, width - step, 1)
        below = pltpu.roll(v, step, 1)
        v = v + jnp.where((lane // step) % 2 == 0, above, below)
        step *= 2
    return v


def packed_moments(values, first_block):
    sums = jnp.sum(values, axis=0, keepdims=True)
    squares = jnp.sum(values * values, axis=0, keepdims=True)
    rows = jnp.concatenate([sums, squares] * 4, axis=0)
    totals = group_total(rows)
    place = lax.broadcasted_iota(jnp.int32, (1, LANES), 1) % GROUP
    packed = jnp.zeros((1, LANES), F32)
    for block in range(values.shape[1] // LANES):
        piece = totals[:, block * LANES : (block + 1) * LANES]
        packed = jnp.where(place == first_block + block, piece[0:1], packed)
        packed = jnp.where(place == BLOCKS + first_block + block, piece[1:2], packed)
    return packed


def moments(packed, population):
    place = lax.broadcasted_iota(jnp.int32, (2 * BLOCKS, LANES), 1) % GROUP
    row = lax.broadcasted_iota(jnp.int32, (2 * BLOCKS, LANES), 0)
    wide = jnp.broadcast_to(packed, (2 * BLOCKS, LANES))
    spread_out = group_total(jnp.where(place == row, wide, 0.0)) / population
    mean = jnp.concatenate([spread_out[k : k + 1] for k in range(BLOCKS)], axis=1)
    square = jnp.concatenate([spread_out[BLOCKS + k : BLOCKS + k + 1] for k in range(BLOCKS)], axis=1)
    variance = jnp.maximum(square - mean * mean, 0.0)
    return mean, lax.rsqrt(variance + EPSILON)


def kernel(
    S, T, C, W,
    x_hbm, g1, g2, wq_hbm, wk_hbm, wv_hbm, wo_hbm, wc_hbm,
    att_out, conv_out,
    x, wq, wk, wv, wo, wc,
    stat1_src, stat1, stat2_src, stat2, gall1, gall2,
    xall, tokens, keyed, valued, att_src, att_in, dsrc, dall, act, part_src, part,
    xload, wsem, send_sem, upsem, downsem, onsem, gsem, s1sem, xsem, s2sem, asem, dsem, psend, psem,
):
    g = lax.axis_index("groups")
    h = lax.axis_index("space")
    t = lax.axis_index("tm")
    c = lax.axis_index("chan")
    n = S * T * C
    me = (h * T + t) * C + c
    half = D // C
    Kc = D // T
    NF = T * C
    other = lax.rem(c + 1, C)

    def to_everyone(act_on):
        def tile(dh):
            row = lax.rem(h + dh, S)
            for dt in range(T):
                for dc in range(C):
                    act_on((g, row, lax.rem(t + dt, T), lax.rem(c + dc, C)))

        pl.loop(1, S, unroll=S <= 4)(tile)
        for dt in range(T):
            for dc in range(C):
                if dt or dc:
                    act_on((g, h, lax.rem(t + dt, T), lax.rem(c + dc, C)))

    first = [
        pltpu.make_async_copy(src, dst, xload.at[i])
        for i, (src, dst) in enumerate([(x_hbm, x), (g1, gall1.at[c]), (g2, gall2.at[c])])
    ]
    for load in first:
        load.start()
    barrier = pltpu.get_barrier_semaphore()

    to_everyone(
        lambda where: pl.semaphore_signal(barrier, inc=1, device_id=where, device_id_type=MESH)
    )

    loads = [
        pltpu.make_async_copy(src, dst, wsem.at[i])
        for i, (src, dst) in enumerate(
            [(wk_hbm, wk), (wq_hbm, wq), (wv_hbm, wv), (wo_hbm, wo), (wc_hbm, wc)]
        )
    ]
    for load in loads:
        load.start()

    for load in first:
        load.wait()
    own = x[...].reshape(C * W, half).astype(F32)
    stat1_src[...] = packed_moments(own, c * (half // LANES))
    stat1[me] = stat1_src[...]
    xall[h * C + c] = x[c, 0]
    pl.semaphore_wait(barrier, n - 1)

    def send_stat(src, dst, sends, recvs):
        to_everyone(
            lambda where: pltpu.make_async_remote_copy(
                src_ref=src, dst_ref=dst.at[me], send_sem=sends, recv_sem=recvs,
                device_id=where, device_id_type=MESH,
            ).start()
        )

    def drain(ref, sem):
        pltpu.make_async_copy(ref, ref, sem).wait()

    send_stat(stat1_src, stat1, send_sem.at[0], s1sem)
    gains = [
        pltpu.make_async_remote_copy(
            src_ref=src, dst_ref=dst.at[c], send_sem=send_sem.at[1 + k], recv_sem=gsem.at[k],
            device_id=(g, h, t, other), device_id_type=MESH,
        )
        for k, (src, dst) in enumerate([(g1, gall1), (g2, gall2)])
    ]
    for copy in gains:
        copy.start()
    def send_x(dh, dc, sem):
        frame = lax.rem(c + dc, C)
        pltpu.make_async_remote_copy(
            src_ref=x.at[frame, 0], dst_ref=xall.at[h * C + c], send_sem=sem, recv_sem=xsem.at[h],
            device_id=(g, h + dh, t, frame), device_id_type=MESH,
        ).start()

    reach = min(REACH, S - 1)
    for dc in range(1, C):
        send_x(0, dc, send_sem.at[3])
    for d in range(reach, 0, -1):

        @pl.when(h + d < S)
        def _():
            for dc in range(C):
                send_x(d, dc, upsem.at[d - 1])

        @pl.when(h >= d)
        def _():
            for dc in range(C):
                send_x(-d, dc, downsem.at[d - 1])

    def slots(r):
        return xall.at[pl.ds(r * C, C)]

    def hand_on(r, to, sem):
        return pltpu.make_async_remote_copy(
            src_ref=slots(r), dst_ref=slots(r), send_sem=sem, recv_sem=xsem.at[r],
            device_id=(g, to, t, c), device_id_type=MESH,
        )

    for d in range(reach, S - 1):

        @pl.when((h >= d) & (h < S - 1))
        def _():
            drain(slots(h - d), xsem.at[h - d])
            hand_on(h - d, h + 1, onsem.at[0, d]).start()

        @pl.when((h + d < S) & (h > 0))
        def _():
            drain(slots(h + d), xsem.at[h + d])
            hand_on(h + d, h - 1, onsem.at[1, d]).start()

    drain(stat1.at[pl.ds(0, n - 1)], s1sem)
    for copy in gains:
        copy.wait()
    population = float(n * W * GROUP)
    mean1, scale1 = moments(jnp.sum(stat1[...], axis=0), population)
    gain1 = jnp.concatenate([gall1[k] for k in range(C)], axis=1)
    gain2 = jnp.concatenate([gall2[k] for k in range(C)], axis=1)

    def row_tokens(r):
        pieces = []
        for k in range(C):
            lanes = slice(k * half, (k + 1) * half)
            value = xall[r * C + k].astype(F32)
            value = (value - mean1[:, lanes]) * scale1[:, lanes] * gain1[:, lanes]
            pieces.append(value.astype(BF16))
        return jnp.concatenate(pieces, axis=1)

    def project(first, stop):
        rows = tokens[first:stop].reshape((stop - first) * W, D)
        shape = (stop - first, W, D)
        keyed[first:stop] = jnp.dot(rows, wk[...], preferred_element_type=F32).astype(BF16).reshape(shape)
        valued[first:stop] = jnp.dot(rows, wv[...], preferred_element_type=F32).astype(BF16).reshape(shape)

    drain(xall.at[pl.ds(0, C - 1)], xsem.at[h])
    mine = row_tokens(h)
    loads[0].wait()
    loads[1].wait()
    loads[2].wait()
    queries = jnp.dot(mine, wq[...], preferred_element_type=F32).astype(BF16)
    tokens[0] = mine

    mirror = (2 * h) // S
    place_h = h + mirror * (S - 1 - 2 * h)
    for k in range(S - 1):
        r = k + (k - place_h + S) // S
        r = r + mirror * (S - 1 - 2 * r)

        @pl.when(jnp.logical_not(((r + reach <= h) & (h < S - 1)) | ((r >= h + reach) & (h > 0))))
        def _():
            drain(slots(r), xsem.at[r])

        tokens[k + 1] = row_tokens(r)

    project(0, S)

    scores = lax.dot_general(
        queries, keyed[...].reshape(S * W, D), (((1,), (1,)), ((), ())), preferred_element_type=F32
    ) * (D ** (-0.5))
    weights = jnp.exp(scores - jnp.max(scores, axis=1, keepdims=True))
    mass = jnp.sum(weights, axis=1, keepdims=True)
    mixed = jnp.dot(weights.astype(BF16), valued[...].reshape(S * W, D), preferred_element_type=F32)
    mixed = (mixed / mass).astype(BF16)
    loads[3].wait()
    attended = jnp.dot(mixed, wo[...], preferred_element_type=F32).astype(BF16)

    source = jnp.concatenate([xall[h * C + k] for k in range(C)], axis=1).astype(F32)
    resid = (source - mean1) + attended.astype(F32)
    for k in range(T):
        dsrc[k] = resid[:, k * Kc : (k + 1) * Kc].astype(BF16)
    for k in range(C):
        att_src[k] = attended[:, k * half : (k + 1) * half]
    stat2_src[...] = packed_moments(resid, 0)
    stat2[me] = stat2_src[...]
    send_stat(stat2_src, stat2, send_sem.at[4], s2sem)

    frame_at = t * C + c

    def send_rows(dh, skip_self):
        for dt in range(T):
            for dc in range(C):
                if skip_self and dt == 0 and dc == 0:
                    continue
                to = lax.rem(t + dt, T)
                pltpu.make_async_remote_copy(
                    src_ref=dsrc.at[to], dst_ref=dall.at[1 - dh, frame_at],
                    send_sem=send_sem.at[6 + dh], recv_sem=dsem.at[1 - dh],
                    device_id=(g, h + dh, to, lax.rem(c + dc, C)), device_id_type=MESH,
                ).start()

    @pl.when(h > 0)
    def _():
        send_rows(-1, False)

    @pl.when(h < S - 1)
    def _():
        send_rows(1, False)

    send_rows(0, True)
    back = pltpu.make_async_remote_copy(
        src_ref=att_src.at[other], dst_ref=att_in, send_sem=send_sem.at[8], recv_sem=asem,
        device_id=(g, h, t, other), device_id_type=MESH,
    )
    back.start()
    dall[1, frame_at] = dsrc[t]
    att_out[c, 0] = att_src[c]
    act[0:2] = jnp.zeros((2,) + act.shape[1:], BF16)

    drain(stat2.at[pl.ds(0, n - 1)], s2sem)
    mean2, scale2 = moments(jnp.sum(stat2[...], axis=0), population)
    factor = scale2 * gain2

    def sliced(v):
        out = v[:, 0:Kc]
        for k in range(1, T):
            out = jnp.where(t == k, v[:, k * Kc : (k + 1) * Kc], out)
        return out

    mean_t = sliced(mean2)
    factor_t = sliced(factor)
    column = lax.broadcasted_iota(jnp.int32, (W, Kc), 0)

    def activate(row):
        @pl.loop(0, NF, unroll=NF <= 4)
        def _(f):
            v = (dall[row, f].astype(F32) - mean_t) * factor_t
            a = v / (1.0 + jnp.exp(-v))
            left = jnp.where(column == 0, 0.0, pltpu.roll(a, 1, 0))
            right = jnp.where(column == W - 1, 0.0, pltpu.roll(a, W - 1, 0))
            for e, piece in enumerate((left, a, right)):
                k = row * 3 + e
                act[f + 2, :, k * Kc : (k + 1) * Kc] = piece.astype(BF16)

    def blank(row):
        act[2:, :, row * 3 * Kc : (row + 1) * 3 * Kc] = jnp.zeros((NF, W, 3 * Kc), BF16)

    drain(dall.at[1, pl.ds(0, NF - 1)], dsem.at[1])
    activate(1)

    @pl.when(h > 0)
    def _():
        drain(dall.at[0], dsem.at[0])
        activate(0)

    @pl.when(h == 0)
    def _():
        blank(0)

    @pl.when(h < S - 1)
    def _():
        drain(dall.at[2], dsem.at[2])
        activate(2)

    @pl.when(h == S - 1)
    def _():
        blank(2)

    loads[4].wait()

    def partial(to):
        total = None
        for a in range(3):
            window = act[pl.ds(to * C + a, C)].reshape(C * W, 9 * Kc)
            product = jnp.dot(window, wc[a], preferred_element_type=F32)
            total = product if total is None else total + product
        return total

    returns = []
    for dt in range(1, T):
        to = lax.rem(t + dt, T)
        part_src[dt - 1] = partial(to).astype(BF16)
        copy = pltpu.make_async_remote_copy(
            src_ref=part_src.at[dt - 1], dst_ref=part.at[dt - 1],
            send_sem=psend.at[dt - 1], recv_sem=psem.at[dt - 1],
            device_id=(g, h, to, c), device_id_type=MESH,
        )
        copy.start()
        returns.append(copy)
    total = partial(t)
    back.wait()
    att_out[other, 0] = att_in[...]

    drain(stat1.at[pl.ds(0, n - 1)], send_sem.at[0])
    drain(xall.at[pl.ds(0, C - 1)], send_sem.at[3])
    for d in range(1, reach + 1):

        @pl.when(h + d < S)
        def _():
            drain(slots(0), upsem.at[d - 1])

        @pl.when(h >= d)
        def _():
            drain(slots(0), downsem.at[d - 1])

    for d in range(reach, S - 1):

        @pl.when((h >= d) & (h < S - 1))
        def _():
            drain(slots(0), onsem.at[0, d])

        @pl.when((h + d < S) & (h > 0))
        def _():
            drain(slots(0), onsem.at[1, d])

    drain(stat2.at[pl.ds(0, n - 1)], send_sem.at[4])
    drain(dall.at[1, pl.ds(0, NF - 1)], send_sem.at[6])

    @pl.when(h > 0)
    def _():
        drain(dall.at[0], send_sem.at[5])

    @pl.when(h < S - 1)
    def _():
        drain(dall.at[2], send_sem.at[7])

    for k, copy in enumerate(returns):
        copy.wait()
        total = total + part[k].astype(F32)
    conv_out[...] = total.reshape(conv_out.shape).astype(BF16)


def hand_over(att_in, conv_in, att_out, conv_out):
    att_out[...] = att_in[...]
    conv_out[...] = conv_in[...]


def on_device(S, T, C, x, g1, g2, wq, wk, wv, wo, wc):
    frames, rows, W, half = x.shape
    assert frames == C and rows == 1 and half * C == D
    Kc = wc.shape[3]
    assert Kc * T == D
    n, NF = S * T * C, T * C
    wc = wc.reshape(3, 9 * Kc, half)
    vmem = pl.BlockSpec(memory_space=pltpu.VMEM)
    hbm = pl.BlockSpec(memory_space=pl.ANY)
    out = jax.ShapeDtypeStruct(x.shape, BF16)
    dma = pltpu.SemaphoreType.DMA
    kept = pltpu.VMEM(x.shape, BF16)
    results = pl.pallas_call(
        functools.partial(kernel, S, T, C, W),
        out_shape=(kept, kept),
        in_specs=[hbm] * 8,
        out_specs=(vmem, vmem),
        scratch_shapes=[
            pltpu.VMEM(x.shape, BF16),
            *[pltpu.VMEM((D, D), BF16)] * 4,
            pltpu.VMEM(wc.shape, BF16),
            pltpu.VMEM((1, LANES), F32),
            pltpu.VMEM((n, 1, LANES), F32),
            pltpu.VMEM((1, LANES), F32),
            pltpu.VMEM((n, 1, LANES), F32),
            pltpu.VMEM((C, 1, half), F32),
            pltpu.VMEM((C, 1, half), F32),
            pltpu.VMEM((S * C, W, half), BF16),
            *[pltpu.VMEM((S, W, D), BF16)] * 3,
            pltpu.VMEM((C, W, half), BF16),
            pltpu.VMEM((W, half), BF16),
            pltpu.VMEM((T, W, Kc), BF16),
            pltpu.VMEM((3, NF, W, Kc), BF16),
            pltpu.VMEM((NF + 2, W, 9 * Kc), BF16),
            pltpu.VMEM((max(T - 1, 1), C * W, half), BF16),
            pltpu.VMEM((max(T - 1, 1), C * W, half), BF16),
            dma((3,)),
            dma((5,)),
            dma((9,)),
            dma((REACH,)),
            dma((REACH,)),
            dma((2, S)),
            dma((2,)),
            dma(()),
            dma((S,)),
            dma(()),
            dma(()),
            dma((3,)),
            dma((max(T - 1, 1),)),
            dma((max(T - 1, 1),)),
        ],
        compiler_params=pltpu.CompilerParams(collective_id=0, has_side_effects=True),
    )(x, g1.reshape(1, half), g2.reshape(1, half), wq, wk, wv, wo, wc)
    return pl.pallas_call(
        hand_over, out_shape=(out, out), in_specs=[vmem] * 2, out_specs=(vmem, vmem),
    )(*[pltpu.with_memory_space_constraint(r, pltpu.VMEM) for r in results])


def solution(mesh):
    S, T, C = mesh.shape["space"], mesh.shape["tm"], mesh.shape["chan"]
    placed = (
        P(("groups", "tm"), "space", None, "chan"),
        P("chan"),
        P("chan"),
        P(),
        P(),
        P(),
        P(),
        P(None, None, None, "tm", "chan"),
    )
    return jax.shard_map(
        functools.partial(on_device, S, T, C),
        mesh=mesh,
        in_specs=placed,
        out_specs=(
            P(("groups", "tm"), "space", None, "chan"),
            P(("groups", "tm"), "space", None, "chan"),
        ),
        check_vma=False,
    )
```
